32 devices in a mesh: dom: 8 (over z, y), case: 4 (over x, core).
Axes of the slice: x: 2, y: 2, z: 4, core: 2. Of those that a mesh axis runs over, the one named last changes fastest.
Arguments:
- dual_ops: float32 [16, 1536, 1536], P('dom')
- modes: bfloat16 [16, 16, 1536], P('dom'), may hold values from -0.15625 to 0.15625
- coarse_rows: float32 [16, 8, 16, 16], P('dom'), may hold values from -1 to 1
- coarse_cols: int32 [16, 8], P('dom'), may hold values from 0 to 15, as said below
- row_perm: int32 [16, 1536], P('dom'), may hold values from 0 to 1535, each once within a row
- iface_size: int32 [16], P('dom'), may hold values from 256 to 768, as said below
- rhs: float32 [16, 768, 512], P('dom', None, 'case'), may hold values from -6 to 6
Outputs:
- solution: float32 [16, 768, 512], P('dom', None, 'case')
- residual: float32 [16, 768, 512], P('dom', None, 'case')
- history: float32 [4, 512], P(None, 'case')
- peak_norm: float32 [4], replicated
The draws below stay inside these ranges and needn't reach their ends.
Inputs may be any that keep to these rules, and one draw needn't show every extreme that they name: `iface_size`: interfaces carry between 256 and 768 multipliers; both ends are reached in every draw. `coarse_cols`: for every subdomain s the first three entries are s, (s - 1) mod 16 and (s + 1) mod 16; the others are any subdomains, repeats allowed. `row_perm`: each row is a permutation of the local rows.
All inputs are finite; a program needn't handle non-finite values.
Results may differ from the reference program's by a relative error of at most 0.0056.
Values may be sent and summed in bfloat16 or wider, within the bound.
A program may use at most 192 MiB of HBM per device.

```python
import jax
import jax.numpy as jnp
from jax import lax

NMAX = 1536
MODES = 16
NB = 8
STEPS = 4
MMAX = 768
MMIN = 256
DOMS = 16
CASES = 512


def draw_dual_ops(key, part):

    def single(position):
        subkey = jax.random.fold_in(jax.random.fold_in(key, 17), position)
        first_key, second_key = jax.random.split(subkey, 2)
        noise = jax.random.normal(first_key, (NMAX, NMAX), jnp.float32) / jnp.sqrt(2.0 * NMAX)
        matrix = noise + noise.T
        diagonal = jax.random.uniform(second_key, (NMAX,), jnp.float32, 3.0, 5.0)
        matrix = matrix + jnp.diag(diagonal)
        return matrix
    return lax.map(single, jnp.arange(DOMS, dtype=jnp.int32))


def draw_iface_size(key, part):
    first_key, second_key, third_key, fourth_key = jax.random.split(jax.random.fold_in(key, 29), 4)
    heavy = jax.random.randint(first_key, (DOMS,), 0, 4) == 0
    higher = jax.random.randint(second_key, (DOMS,), 3 * MMAX // 4, MMAX + 1)
    lower = jax.random.randint(third_key, (DOMS,), MMIN, MMAX // 2 + 1)
    sizes = jnp.where(heavy, higher, lower)
    spots = jax.random.randint(fourth_key, (2,), 0, DOMS)
    sizes = sizes.at[spots[0]].set(MMAX)
    sizes = sizes.at[(spots[0] + 1 + spots[1] % (DOMS - 1)) % DOMS].set(MMIN)
    return sizes.astype(jnp.int32)


def draw_coarse_cols(key, part):
    owners = jnp.arange(DOMS, dtype=jnp.int32)
    extra = jax.random.randint(jax.random.fold_in(key, 41), (DOMS, NB - 3), 0, DOMS)
    columns = [owners[:, None], ((owners - 1) % DOMS)[:, None], ((owners + 1) % DOMS)[:, None], extra]
    return jnp.concatenate(columns, axis=1).astype(jnp.int32)


def block_levels(stream_key, dims, cuts, smallest, high):
    factor_of, own = 1.0, jax.random.fold_in(stream_key, 6)
    for axis_at, parts in cuts:
        heights = jnp.exp(jax.random.uniform(jax.random.fold_in(own, axis_at), (parts,), jnp.float32, smallest / len(cuts), high / len(cuts)))
        factor_of = factor_of * jnp.repeat(heights, dims[axis_at] // parts).reshape([-1 if axis == axis_at else 1 for axis in range(len(dims))])
    return factor_of


def gaussian(key, shape, deviation, reach, shards=(), kind=jnp.bfloat16):
    array = jax.random.normal(key, shape, jnp.float32) * deviation
    if len(shards) > 0:
        array = block_levels(key, shape, shards, -0.22, 0.18) * array
    return jnp.clip(array, min=-reach, max=reach).astype(kind)


def setup_inputs(seed: int = 0) -> dict:
    streams_of = jax.random.split(jax.random.key(seed), 8)
    dual_ops = draw_dual_ops(jax.random.fold_in(streams_of[7], 71), 0)
    modes = gaussian(streams_of[1], (DOMS, MODES, NMAX), NMAX ** -0.5, 0.15625, ((0, 8),))
    coarse_rows = gaussian(streams_of[2], (DOMS, NB, MODES, MODES), 0.15, 1.0, ((0, 8),), jnp.float32)
    coarse_cols = draw_coarse_cols(jax.random.fold_in(streams_of[7], 71), 0)
    row_perm = jax.vmap(lambda own: jax.random.permutation(own, NMAX))(jax.random.split(streams_of[4], DOMS)).reshape((DOMS, NMAX)).astype(jnp.int32)
    iface_size = draw_iface_size(jax.random.fold_in(streams_of[7], 71), 0)
    rhs = gaussian(streams_of[6], (DOMS, MMAX, CASES), 1.0, 6.0, ((0, 8), (2, 4)), jnp.float32)
    return dict(dual_ops=dual_ops, modes=modes, coarse_rows=coarse_rows, coarse_cols=coarse_cols, row_perm=row_perm, iface_size=iface_size, rhs=rhs)


low_bound = 2.0
high_bound = 14.0
epsilon = 1e-06
highest = lax.Precision.HIGHEST

def pick_rows(source, rows_index):
    return jax.vmap(lambda block_rows, chosen: block_rows[chosen])(source, rows_index)

def build_local(vector, inverse):
    left_side = jnp.roll(vector, 1, axis=0)
    return pick_rows(jnp.concatenate([-left_side, vector], axis=1), inverse)

def assemble(local_rows, row_perm, live_mask):
    combined = pick_rows(local_rows, row_perm)
    half_width = combined.shape[1] // 2
    return (combined[:, half_width:] - jnp.roll(combined[:, :half_width], -1, axis=0)) * live_mask

def coarse(local_rows, modes_wide, coarse_rows, coarse_cols):
    coefficients = jnp.einsum('sjn,snc->sjc', modes_wide, local_rows, precision=highest).astype(jnp.bfloat16)
    coefficients = lax.optimization_barrier(coefficients)
    picked = coefficients[coarse_cols].astype(jnp.float32)
    amounts = jnp.einsum('sqij,sqjc->sic', coarse_rows, picked, precision=highest)
    return jnp.einsum('sjn,sjc->snc', modes_wide, amounts, precision=highest)

def reference(dual_ops, modes, coarse_rows, coarse_cols, row_perm, iface_size, rhs):
    half_width = rhs.shape[1]
    live_mask = (jnp.arange(half_width, dtype=jnp.int32)[None, :] < iface_size[:, None]).astype(jnp.float32)[:, :, None]
    counter = jnp.broadcast_to(jnp.arange(row_perm.shape[1], dtype=jnp.int32)[None, :], row_perm.shape)
    inverse = jax.vmap(lambda ordering, values: jnp.zeros_like(ordering).at[ordering].set(values))(row_perm, counter)
    modes_wide = modes.astype(jnp.float32)

    def project(vector):
        local_rows = build_local(vector, inverse)
        return vector - assemble(coarse(local_rows, modes_wide, coarse_rows, coarse_cols), row_perm, live_mask)

    def operator(vector):
        local_rows = build_local(vector, inverse)
        product = jnp.einsum('snm,smc->snc', dual_ops, local_rows, precision=highest)
        return assemble(product, row_perm, live_mask)
    centre = 0.5 * (high_bound + low_bound)
    radius = 0.5 * (high_bound - low_bound)
    spread_ratio = centre / radius
    ratio_now = 1.0 / spread_ratio
    residual = project(rhs * live_mask)
    direction = residual / centre
    solution = jnp.zeros_like(rhs)
    norm_list = []
    for turn_index in range(STEPS):
        solution = solution + direction
        residual = residual - project(operator(direction))
        norm_list.append(jnp.sqrt(lax.optimization_barrier(jnp.sum(residual * residual, axis=(0, 1))) + epsilon))
        if turn_index + 1 < STEPS:
            ratio_next = 1.0 / (2.0 * spread_ratio - ratio_now)
            direction = ratio_next * ratio_now * direction + 2.0 * ratio_next / radius * residual
            ratio_now = ratio_next
    history = jnp.stack(norm_list)
    return (solution, residual, history, lax.optimization_barrier(jnp.max(history, axis=1)))
```

```python
import functools

import jax
import jax.numpy as jnp
from jax import lax
from jax.experimental import pallas as pl
from jax.experimental.pallas import tpu as pltpu
from jax.sharding import PartitionSpec as P

STEPS = 4


low_bound = 2.0
high_bound = 14.0
epsilon = 1e-06
highest = lax.Precision.HIGHEST
f32, bf16 = jnp.float32, jnp.bfloat16


def from_behind(block, axis, distance):
    devices = range(lax.axis_size(axis))
    route = [((i - distance) % len(devices), i) for i in devices]
    return lax.ppermute(block, axis, route)


def gather_kernel(axes, sizes, x_ref, out_ref, own_sem, send_sem, recv_sem):
    me = [lax.axis_index(axis) for axis in axes]

    def flat(position):
        index = 0
        for at, size in zip(position, sizes):
            index = index * size + at
        return index

    offsets = [()]
    for size in sizes:
        offsets = [o + (k,) for o in offsets for k in range(size)]
    targets = [
        {axis: lax.rem(at + k, size) for axis, at, k, size in zip(axes, me, offset, sizes)}
        for offset in offsets[1:]
    ]
    barrier = pltpu.get_barrier_semaphore()
    for target in targets:
        pl.semaphore_signal(
            barrier, inc=1, device_id=target, device_id_type=pl.DeviceIdType.MESH
        )
    own = pltpu.make_async_copy(x_ref, out_ref.at[flat(me)], own_sem)
    own.start()
    pl.semaphore_wait(barrier, len(targets))
    copies = []
    for k, target in enumerate(targets):
        copy = pltpu.make_async_remote_copy(
            src_ref=x_ref,
            dst_ref=out_ref.at[flat(me)],
            send_sem=send_sem.at[k],
            recv_sem=recv_sem.at[k],
            device_id=target,
            device_id_type=pl.DeviceIdType.MESH,
        )
        copy.start()
        copies.append(copy)
    own.wait()
    for copy in copies:
        copy.wait()


def push_gather(block, axes, collective_id):
    sizes = tuple(lax.axis_size(axis) for axis in axes)
    count = 1
    for size in sizes:
        count *= size
    return pl.pallas_call(
        functools.partial(gather_kernel, axes, sizes),
        out_shape=jax.ShapeDtypeStruct((count,) + block.shape, block.dtype),
        in_specs=[pl.BlockSpec(memory_space=pltpu.VMEM)],
        out_specs=pl.BlockSpec(memory_space=pltpu.VMEM),
        scratch_shapes=[
            pltpu.SemaphoreType.DMA,
            pltpu.SemaphoreType.DMA((count - 1,)),
            pltpu.SemaphoreType.DMA((count - 1,)),
        ],
        compiler_params=pltpu.CompilerParams(collective_id=collective_id, has_side_effects=True),
    )(block)


def put_split(ref, rows, value):
    width = value.shape[1]
    high = value.astype(bf16)
    ref[rows, :width] = high
    ref[rows, width:] = (value - high.astype(f32)).astype(bf16)


def joined_halves(pair):
    width = pair.shape[1] // 2
    return pair[:, :width] + pair[:, width:]


def apply_kernel(sub, d_ref, row_ref, col_ref, a_ref, lower_ref, upper_ref, xs, xl, ys):
    step = pl.program_id(0)
    depth, size = a_ref.shape[1:]
    half = size // 2

    @pl.when(step == 0)
    def _():
        put_split(xs, pl.ds(0, half), -d_ref[sub])
        put_split(xs, pl.ds(half, half), d_ref[sub + 1])
        spots = row_ref[...]

        @pl.loop(0, size // depth)
        def _(b):
            start = pl.multiple_of(b * depth, depth)
            want = lax.broadcasted_iota(jnp.int32, (depth, size), 0) + start
            table = jnp.where(want == spots, 1.0, 0.0).astype(bf16)
            xl[pl.ds(start, depth), :] = jnp.dot(
                table, xs[...], preferred_element_type=f32
            ).astype(bf16)

    block = a_ref[0]
    high = block.astype(bf16)
    low = (block - high.astype(f32)).astype(bf16)
    vector = xl[...]
    pair = jnp.dot(high, vector, preferred_element_type=f32) + jnp.dot(
        low, vector, preferred_element_type=f32
    )
    put_split(ys, pl.ds(pl.multiple_of(step * depth, depth), depth), joined_halves(pair))

    @pl.when(step == size // depth - 1)
    def _():
        for side, out_ref in enumerate((lower_ref, upper_ref)):

            @pl.loop(0, half // depth)
            def _(b):
                start = pl.multiple_of(b * depth, depth)
                spots = col_ref[pl.ds(side * half + start, depth), :]
                lane = lax.broadcasted_iota(jnp.int32, (depth, size), 1)
                table = jnp.where(lane == spots, 1.0, 0.0).astype(bf16)
                out_ref[pl.ds(start, depth), :] = joined_halves(
                    jnp.dot(table, ys[...], preferred_element_type=f32)
                )


def apply_operator(direction, row_perm, col_perm, dual_ops, sub):
    size = dual_ops.shape[1]
    half, width = direction.shape[1:]
    depth = next(d for d in (256, 128, 64, 32, 16) if half % d == 0)
    return pl.pallas_call(
        functools.partial(apply_kernel, sub),
        grid=(size // depth,),
        out_shape=[jax.ShapeDtypeStruct((half, width), f32)] * 2,
        in_specs=[
            pl.BlockSpec(direction.shape, lambda i: (0, 0, 0)),
            pl.BlockSpec((None, 1, size), lambda i: (sub, 0, 0)),
            pl.BlockSpec((None, size, 1), lambda i: (sub, 0, 0)),
            pl.BlockSpec((1, depth, size), lambda i: (sub, i, 0)),
        ],
        out_specs=[pl.BlockSpec((half, width), lambda i: (0, 0))] * 2,
        scratch_shapes=[pltpu.VMEM((size, 2 * width), bf16)] * 3,
        cost_estimate=pl.CostEstimate(
            flops=16 * size * size * width, bytes_accessed=4 * size * size, transcendentals=0
        ),
        compiler_params=pltpu.CompilerParams(vmem_limit_bytes=40 * 2**20),
    )(direction, row_perm, col_perm, dual_ops)


def split(value, axis):
    high = lax.reduce_precision(value, 8, 7)
    return jnp.concatenate([high.astype(bf16), (value - high).astype(bf16)], axis=axis)


def unsplit(pair):
    width = pair.shape[-1] // 2
    return pair[..., :width] + pair[..., width:]


def shards(dual_ops, modes, coarse_rows, coarse_cols, row_perm, iface_size, rhs):
    sub_count, half_width, case_count = rhs.shape
    size = 2 * half_width
    mode_count = modes.shape[1]
    dom_count = lax.axis_size("dom") * sub_count
    row_view = row_perm[:, None, :]
    col_view = row_perm[:, :, None]
    block_count = coarse_cols.shape[1]
    int_pack = jnp.concatenate([coarse_cols, iface_size[:, None]], axis=1)
    live_own = (
        lax.broadcasted_iota(jnp.int32, (sub_count, half_width), 1) < iface_size[:, None]
    ).astype(f32)[:, :, None]
    start_vector = rhs * live_own
    prior_rim = from_behind(start_vector[-1], "dom", 1)
    prior_ints = from_behind(int_pack[-1], "dom", 1)
    next_ints = from_behind(int_pack[0], "dom", -1)
    permutation = (
        row_perm[:, :, None] == lax.broadcasted_iota(jnp.int32, (1, 1, size), 2)
    ).astype(bf16)
    slot_modes = jnp.einsum("sjn,skn->sjk", modes, permutation, preferred_element_type=f32).astype(
        bf16
    )
    prior_modes = from_behind(slot_modes[-1], "dom", 1)
    next_modes = from_behind(slot_modes[0], "dom", -1)
    prior_blocks = from_behind(coarse_rows[-1], "dom", 1)
    next_blocks = from_behind(coarse_rows[0], "dom", -1)
    ext_ints = jnp.concatenate([prior_ints[None], int_pack, next_ints[None]], axis=0)
    ext_cols = ext_ints[:, :block_count]
    ext_size = ext_ints[:-1, block_count]
    ext_modes = jnp.concatenate([prior_modes[None], slot_modes, next_modes[None]], axis=0)
    ext_blocks = jnp.concatenate([prior_blocks[None], coarse_rows, next_blocks[None]], axis=0)
    live = (
        lax.broadcasted_iota(jnp.int32, (sub_count + 1, half_width), 1) < ext_size[:, None]
    ).astype(f32)[:, :, None]
    column_table = (
        ext_cols[:, :, None] == lax.broadcasted_iota(jnp.int32, (1, 1, dom_count), 2)
    ).astype(f32)
    coarse = jnp.einsum("sqij,sqd->sidj", ext_blocks, column_table, precision=highest).reshape(
        (sub_count + 2) * mode_count, dom_count * mode_count
    )
    fit_modes = jnp.concatenate([-slot_modes[:, :, :half_width], slot_modes[:, :, half_width:]], 2)
    join_modes = jnp.concatenate(
        [ext_modes[:-1, :, half_width:], -ext_modes[1:, :, :half_width]], axis=1
    )

    def correction_of(vector):
        pairs = split(vector, 2)
        locals_ = jnp.concatenate([pairs[:-1], pairs[1:]], axis=1)
        coefficients = unsplit(
            jnp.einsum("sjn,snc->sjc", fit_modes, locals_, preferred_element_type=f32)
        ).astype(bf16)
        everyone = push_gather(coefficients, ("dom",), 1).reshape(
            dom_count * mode_count, case_count
        )
        amounts = jnp.dot(coarse, everyone.astype(f32), precision=highest)
        amounts = split(amounts, 1).reshape(sub_count + 2, mode_count, 2 * case_count)
        amounts = jnp.concatenate([amounts[:-1], amounts[1:]], axis=1)
        return live * unsplit(
            jnp.einsum("sjn,sjc->snc", join_modes, amounts, preferred_element_type=f32)
        )

    centre = 0.5 * (high_bound + low_bound)
    radius = 0.5 * (high_bound - low_bound)
    spread_ratio = centre / radius
    ratio_now = 1.0 / spread_ratio
    residual = jnp.concatenate([prior_rim[None], start_vector], axis=0)
    residual = residual - correction_of(residual)
    direction = residual / centre
    solution = jnp.zeros_like(rhs)
    sums = []
    for turn_index in range(STEPS):
        solution = solution + direction[1:]
        lowers, uppers = [None] * sub_count, [None] * sub_count
        order = [sub_count - 1] + list(range(sub_count - 1))
        for sub in order:
            lowers[sub], uppers[sub] = apply_operator(direction, row_view, col_view, dual_ops, sub)
        uppers = [from_behind(uppers[-1], "dom", 1)] + uppers
        lowers = lowers + [from_behind(lowers[0], "dom", -1)]
        mapped = jnp.stack([u - l for u, l in zip(uppers, lowers)]) * live
        residual = residual - (mapped - correction_of(mapped))
        sums.append(jnp.sum(residual[1:] * residual[1:], axis=(0, 1)))
        if turn_index + 1 < STEPS:
            ratio_next = 1.0 / (2.0 * spread_ratio - ratio_now)
            direction = ratio_next * ratio_now * direction + 2.0 * ratio_next / radius * residual
            ratio_now = ratio_next
    rows = -(-STEPS // 8) * 8
    pack = jnp.zeros((rows, case_count), f32).at[:STEPS].set(jnp.stack(sums))
    cases = lax.axis_size("case")
    everyone = push_gather(pack, ("dom", "case"), 2).reshape(-1, cases, rows, case_count)
    norms = jnp.sqrt(jnp.sum(everyone, axis=0)[:, :STEPS] + epsilon)
    history = lax.dynamic_index_in_dim(norms, lax.axis_index("case"), 0, keepdims=False)
    peak_norm = jnp.max(norms, axis=(0, 2))
    return (solution, residual[1:], history, peak_norm)


def solution(mesh):
    in_specs = (
        P("dom", None, None),
        P("dom", None, None),
        P("dom", None, None, None),
        P("dom", None),
        P("dom", None),
        P("dom"),
        P("dom", None, "case"),
    )
    out_specs = (P("dom", None, "case"), P("dom", None, "case"), P(None, "case"), P())
    return jax.shard_map(shards, mesh=mesh, in_specs=in_specs, out_specs=out_specs, check_vma=False)
```

```python
import functools

import jax
import jax.numpy as jnp
from jax import lax
from jax.experimental import pallas as pl
from jax.experimental.pallas import tpu as pltpu
from jax.sharding import PartitionSpec as P

STEPS = 4


low_bound = 2.0
high_bound = 14.0
epsilon = 1e-06
highest = lax.Precision.HIGHEST
f32, bf16 = jnp.float32, jnp.bfloat16


def from_behind(block, axis, distance):
    devices = range(lax.axis_size(axis))
    route = [((i - distance) % len(devices), i) for i in devices]
    return lax.ppermute(block, axis, route)


def gather_kernel(axes, sizes, x_ref, out_ref, own_sem, send_sem, recv_sem):
    me = [lax.axis_index(axis) for axis in axes]

    def flat(position):
        index = 0
        for at, size in zip(position, sizes):
            index = index * size + at
        return index

    offsets = [()]
    for size in sizes:
        offsets = [o + (k,) for o in offsets for k in range(size)]
    targets = [
        {axis: lax.rem(at + k, size) for axis, at, k, size in zip(axes, me, offset, sizes)}
        for offset in offsets[1:]
    ]
    barrier = pltpu.get_barrier_semaphore()
    for target in targets:
        pl.semaphore_signal(
            barrier, inc=1, device_id=target, device_id_type=pl.DeviceIdType.MESH
        )
    own = pltpu.make_async_copy(x_ref, out_ref.at[flat(me)], own_sem)
    own.start()
    pl.semaphore_wait(barrier, len(targets))
    copies = []
    for k, target in enumerate(targets):
        copy = pltpu.make_async_remote_copy(
            src_ref=x_ref,
            dst_ref=out_ref.at[flat(me)],
            send_sem=send_sem.at[k],
            recv_sem=recv_sem.at[k],
            device_id=target,
            device_id_type=pl.DeviceIdType.MESH,
        )
        copy.start()
        copies.append(copy)
    own.wait()
    for copy in copies:
        copy.wait()


def push_gather(block, axes, collective_id):
    sizes = tuple(lax.axis_size(axis) for axis in axes)
    count = 1
    for size in sizes:
        count *= size
    return pl.pallas_call(
        functools.partial(gather_kernel, axes, sizes),
        out_shape=jax.ShapeDtypeStruct((count,) + block.shape, block.dtype),
        in_specs=[pl.BlockSpec(memory_space=pltpu.VMEM)],
        out_specs=pl.BlockSpec(memory_space=pltpu.VMEM),
        scratch_shapes=[
            pltpu.SemaphoreType.DMA,
            pltpu.SemaphoreType.DMA((count - 1,)),
            pltpu.SemaphoreType.DMA((count - 1,)),
        ],
        compiler_params=pltpu.CompilerParams(collective_id=collective_id, has_side_effects=True),
    )(block)


def put_split(ref, rows, value):
    width = value.shape[1]
    high = value.astype(bf16)
    ref[rows, :width] = high
    ref[rows, width:] = (value - high.astype(f32)).astype(bf16)


def joined_halves(pair):
    width = pair.shape[1] // 2
    return pair[:, :width] + pair[:, width:]


def setup_kernel(row_ref, col_ref, a_ref, out_ref, diagonal_ref, rest, table, diagonal):
    depth, size = out_ref.shape

    @pl.when(pl.program_id(1) == 0)
    def _():
        spots = row_ref[...]
        diagonal[...] = jnp.zeros_like(diagonal)

        @pl.loop(0, size // depth)
        def _(b):
            start = pl.multiple_of(b * depth, depth)
            row = lax.broadcasted_iota(jnp.int32, (depth, size), 0) + start
            same = row == lax.broadcasted_iota(jnp.int32, (depth, size), 1)
            block = a_ref[pl.ds(start, depth), :]
            diagonal[...] += jnp.sum(jnp.where(same, block, 0.0), axis=0, keepdims=True)
            rest[pl.ds(start, depth), :] = jnp.where(same, 0.0, block).astype(bf16)
            table[pl.ds(start, depth), :] = jnp.where(row == spots, 1.0, 0.0).astype(bf16)

    hit = lax.broadcasted_iota(jnp.int32, (depth, size), 1) == col_ref[...]
    diagonal_ref[...] = jnp.sum(jnp.where(hit, diagonal[...], 0.0), axis=1, keepdims=True)
    picked = jnp.dot(
        jnp.where(hit, 1.0, 0.0).astype(bf16), rest[...], preferred_element_type=f32
    ).astype(bf16)
    out_ref[...] = jnp.dot(picked, table[...], preferred_element_type=f32).astype(bf16)


def slot_operator(dual_ops, row_perm, col_perm, sub):
    size = dual_ops.shape[1]
    depth = next(d for d in (256, 128, 64, 32, 16) if size % d == 0)
    return pl.pallas_call(
        setup_kernel,
        grid=(1, size // depth),
        out_shape=[
            jax.ShapeDtypeStruct((size, size), bf16),
            jax.ShapeDtypeStruct((size, 1), f32),
        ],
        in_specs=[
            pl.BlockSpec((None, 1, size), lambda s, i: (sub, 0, 0)),
            pl.BlockSpec((None, depth, 1), lambda s, i: (sub, i, 0)),
            pl.BlockSpec((None, size, size), lambda s, i: (sub, 0, 0)),
        ],
        out_specs=[
            pl.BlockSpec((depth, size), lambda s, i: (i, 0)),
            pl.BlockSpec((depth, 1), lambda s, i: (i, 0)),
        ],
        scratch_shapes=[
            pltpu.VMEM((size, size), bf16),
            pltpu.VMEM((size, size), bf16),
            pltpu.VMEM((1, size), f32),
        ],
        cost_estimate=pl.CostEstimate(
            flops=4 * size**3, bytes_accessed=6 * size * size, transcendentals=0
        ),
        compiler_params=pltpu.CompilerParams(vmem_limit_bytes=56 * 2**20),
    )(row_perm, col_perm, dual_ops)


def apply_kernel(sub, d_ref, a_ref, lower_ref, upper_ref, lower_low_ref, upper_low_ref, xs):
    half = a_ref.shape[0]
    step = pl.program_id(0)

    @pl.when(step == 0)
    def _():
        put_split(xs, pl.ds(0, half), -d_ref[sub])
        put_split(xs, pl.ds(half, half), d_ref[sub + 1])

    outs = ((lower_ref, lower_low_ref), (upper_ref, upper_low_ref))
    depth = half // 3 if half % 48 == 0 else half
    for side, (wide, narrow) in enumerate(outs):

        @pl.when(step == side)
        def _():
            for start in range(0, half, depth):
                rows = pl.ds(start, depth)
                value = joined_halves(
                    jnp.dot(a_ref[rows, :], xs[...], preferred_element_type=f32)
                )
                wide[rows, :] = value
                narrow[rows, :] = value.astype(bf16)


def apply_operator(direction, operator, sub):
    size = operator.shape[0]
    half, width = direction.shape[1:]
    return pl.pallas_call(
        functools.partial(apply_kernel, sub),
        grid=(2,),
        out_shape=[jax.ShapeDtypeStruct((half, width), f32)] * 2
        + [jax.ShapeDtypeStruct((half, width), bf16)] * 2,
        in_specs=[
            pl.BlockSpec(direction.shape, lambda i: (0, 0, 0)),
            pl.BlockSpec((half, size), lambda i: (i, 0)),
        ],
        out_specs=[pl.BlockSpec((half, width), lambda i: (0, 0))] * 4,
        scratch_shapes=[pltpu.VMEM((size, 2 * width), bf16)],
        cost_estimate=pl.CostEstimate(
            flops=4 * size * size * width, bytes_accessed=2 * size * size, transcendentals=0
        ),
        compiler_params=pltpu.CompilerParams(vmem_limit_bytes=24 * 2**20),
    )(direction, operator)


def split(value, axis):
    high = lax.reduce_precision(value, 8, 7)
    return jnp.concatenate([high.astype(bf16), (value - high).astype(bf16)], axis=axis)


def unsplit(pair):
    width = pair.shape[-1] // 2
    return pair[..., :width] + pair[..., width:]


def shards(dual_ops, modes, coarse_rows, coarse_cols, row_perm, iface_size, rhs):
    sub_count, half_width, case_count = rhs.shape
    size = 2 * half_width
    mode_count = modes.shape[1]
    dom_count = lax.axis_size("dom") * sub_count
    row_view = row_perm[:, None, :]
    col_view = row_perm[:, :, None]
    block_count = coarse_cols.shape[1]
    int_pack = jnp.concatenate([coarse_cols, iface_size[:, None]], axis=1)
    live_own = (
        lax.broadcasted_iota(jnp.int32, (sub_count, half_width), 1) < iface_size[:, None]
    ).astype(f32)[:, :, None]
    start_vector = rhs * live_own
    prior_rim = from_behind(start_vector[-1], "dom", 1)
    prior_ints = from_behind(int_pack[-1], "dom", 1)
    next_ints = from_behind(int_pack[0], "dom", -1)
    permutation = (
        row_perm[:, :, None] == lax.broadcasted_iota(jnp.int32, (1, 1, size), 2)
    ).astype(bf16)
    slot_modes = jnp.einsum("sjn,skn->sjk", modes, permutation, preferred_element_type=f32).astype(
        bf16
    )
    prior_modes = from_behind(slot_modes[-1], "dom", 1)
    next_modes = from_behind(slot_modes[0], "dom", -1)
    prior_blocks = from_behind(coarse_rows[-1], "dom", 1)
    next_blocks = from_behind(coarse_rows[0], "dom", -1)
    ext_ints = jnp.concatenate([prior_ints[None], int_pack, next_ints[None]], axis=0)
    ext_cols = ext_ints[:, :block_count]
    ext_size = ext_ints[:-1, block_count]
    ext_modes = jnp.concatenate([prior_modes[None], slot_modes, next_modes[None]], axis=0)
    ext_blocks = jnp.concatenate([prior_blocks[None], coarse_rows, next_blocks[None]], axis=0)
    live = (
        lax.broadcasted_iota(jnp.int32, (sub_count + 1, half_width), 1) < ext_size[:, None]
    ).astype(f32)[:, :, None]
    operators, diagonals = zip(
        *[slot_operator(dual_ops, row_view, col_view, sub) for sub in range(sub_count)]
    )
    upper_diagonals = [d[half_width:, 0] for d in diagonals]
    lower_diagonals = [d[:half_width, 0] for d in diagonals]
    upper_diagonals = [from_behind(upper_diagonals[-1], "dom", 1)] + upper_diagonals
    lower_diagonals = lower_diagonals + [from_behind(lower_diagonals[0], "dom", -1)]
    diagonal = jnp.stack(upper_diagonals) + jnp.stack(lower_diagonals)
    diagonal = diagonal[:, :, None]
    column_table = (
        ext_cols[:, :, None] == lax.broadcasted_iota(jnp.int32, (1, 1, dom_count), 2)
    ).astype(f32)
    coarse = jnp.einsum("sqij,sqd->sidj", ext_blocks, column_table, precision=highest).reshape(
        (sub_count + 2) * mode_count, dom_count * mode_count
    )
    fit_modes = jnp.concatenate([-slot_modes[:, :, :half_width], slot_modes[:, :, half_width:]], 2)
    join_modes = jnp.concatenate(
        [ext_modes[:-1, :, half_width:], -ext_modes[1:, :, :half_width]], axis=1
    )

    def correction_of(vector):
        pairs = split(vector, 2)
        locals_ = jnp.concatenate([pairs[:-1], pairs[1:]], axis=1)
        coefficients = unsplit(
            jnp.einsum("sjn,snc->sjc", fit_modes, locals_, preferred_element_type=f32)
        ).astype(bf16)
        everyone = push_gather(coefficients, ("dom",), 1).reshape(
            dom_count * mode_count, case_count
        )
        amounts = jnp.dot(coarse, everyone.astype(f32), precision=highest)
        amounts = split(amounts, 1).reshape(sub_count + 2, mode_count, 2 * case_count)
        amounts = jnp.concatenate([amounts[:-1], amounts[1:]], axis=1)
        return live * unsplit(
            jnp.einsum("sjn,sjc->snc", join_modes, amounts, preferred_element_type=f32)
        )

    centre = 0.5 * (high_bound + low_bound)
    radius = 0.5 * (high_bound - low_bound)
    spread_ratio = centre / radius
    ratio_now = 1.0 / spread_ratio
    residual = jnp.concatenate([prior_rim[None], start_vector], axis=0)
    residual = residual - correction_of(residual)
    direction = residual / centre
    solution = jnp.zeros_like(rhs)
    sums = []
    for turn_index in range(STEPS):
        solution = solution + direction[1:]
        lowers, uppers = [None] * sub_count, [None] * sub_count
        order = [sub_count - 1] + list(range(sub_count - 1))
        for sub in order:
            lower, upper, lower_low, upper_low = apply_operator(direction, operators[sub], sub)
            lowers[sub], uppers[sub] = lower, upper
            if sub == sub_count - 1:
                rim_up = from_behind(upper_low, "dom", 1).astype(f32)
            if sub == 0:
                rim_low = from_behind(lower_low, "dom", -1).astype(f32)
        uppers = [rim_up] + uppers
        lowers = lowers + [rim_low]
        rest = jnp.stack([u - l for u, l in zip(uppers, lowers)])
        mapped = (diagonal * direction + rest) * live
        residual = residual - (mapped - correction_of(mapped))
        sums.append(jnp.sum(residual[1:] * residual[1:], axis=(0, 1)))
        if turn_index + 1 < STEPS:
            ratio_next = 1.0 / (2.0 * spread_ratio - ratio_now)
            direction = ratio_next * ratio_now * direction + 2.0 * ratio_next / radius * residual
            ratio_now = ratio_next
    rows = -(-STEPS // 8) * 8
    pack = jnp.zeros((rows, case_count), f32).at[:STEPS].set(jnp.stack(sums))
    cases = lax.axis_size("case")
    everyone = push_gather(pack, ("dom", "case"), 2).reshape(-1, cases, rows, case_count)
    norms = jnp.sqrt(jnp.sum(everyone, axis=0)[:, :STEPS] + epsilon)
    history = lax.dynamic_index_in_dim(norms, lax.axis_index("case"), 0, keepdims=False)
    peak_norm = jnp.max(norms, axis=(0, 2))
    return (solution, residual[1:], history, peak_norm)


def solution(mesh):
    in_specs = (
        P("dom", None, None),
        P("dom", None, None),
        P("dom", None, None, None),
        P("dom", None),
        P("dom", None),
        P("dom"),
        P("dom", None, "case"),
    )
    out_specs = (P("dom", None, "case"), P("dom", None, "case"), P(None, "case"), P())
    return jax.shard_map(shards, mesh=mesh, in_specs=in_specs, out_specs=out_specs, check_vma=False)
```

```python
import functools

import jax
import jax.numpy as jnp
from jax import lax
from jax.experimental import pallas as pl
from jax.experimental.pallas import tpu as pltpu
from jax.sharding import PartitionSpec as P

STEPS = 4


low_bound = 2.0
high_bound = 14.0
epsilon = 1e-06
highest = lax.Precision.HIGHEST
f32, bf16 = jnp.float32, jnp.bfloat16


def from_behind(block, axis, distance):
    devices = range(lax.axis_size(axis))
    route = [((i - distance) % len(devices), i) for i in devices]
    return lax.ppermute(block, axis, route)


def gather_kernel(axes, sizes, x_ref, out_ref, own_sem, send_sem, recv_sem):
    me = [lax.axis_index(axis) for axis in axes]

    def flat(position):
        index = 0
        for at, size in zip(position, sizes):
            index = index * size + at
        return index

    offsets = [()]
    for size in sizes:
        offsets = [o + (k,) for o in offsets for k in range(size)]
    targets = [
        {axis: lax.rem(at + k, size) for axis, at, k, size in zip(axes, me, offset, sizes)}
        for offset in offsets[1:]
    ]
    barrier = pltpu.get_barrier_semaphore()
    for target in targets:
        pl.semaphore_signal(
            barrier, inc=1, device_id=target, device_id_type=pl.DeviceIdType.MESH
        )
    own = pltpu.make_async_copy(x_ref, out_ref.at[flat(me)], own_sem)
    own.start()
    pl.semaphore_wait(barrier, len(targets))
    copies = []
    for k, target in enumerate(targets):
        copy = pltpu.make_async_remote_copy(
            src_ref=x_ref,
            dst_ref=out_ref.at[flat(me)],
            send_sem=send_sem.at[k],
            recv_sem=recv_sem.at[k],
            device_id=target,
            device_id_type=pl.DeviceIdType.MESH,
        )
        copy.start()
        copies.append(copy)
    own.wait()
    for copy in copies:
        copy.wait()


def push_gather(block, axes, collective_id):
    sizes = tuple(lax.axis_size(axis) for axis in axes)
    count = 1
    for size in sizes:
        count *= size
    return pl.pallas_call(
        functools.partial(gather_kernel, axes, sizes),
        out_shape=jax.ShapeDtypeStruct((count,) + block.shape, block.dtype),
        in_specs=[pl.BlockSpec(memory_space=pltpu.VMEM)],
        out_specs=pl.BlockSpec(memory_space=pltpu.VMEM),
        scratch_shapes=[
            pltpu.SemaphoreType.DMA,
            pltpu.SemaphoreType.DMA((count - 1,)),
            pltpu.SemaphoreType.DMA((count - 1,)),
        ],
        compiler_params=pltpu.CompilerParams(collective_id=collective_id, has_side_effects=True),
    )(block)


def exchange_kernel(
    count, part_ref, share_ref, up_ref, low_ref, all_ref, up_in, low_in, shares,
    share_send, share_recv, rim_send, rim_recv, send_sem, recv_sem
):
    me = lax.axis_index("dom")
    others = [{"dom": lax.rem(me + k, count)} for k in range(1, count)]
    barrier = pltpu.get_barrier_semaphore()
    for target in others:
        pl.semaphore_signal(
            barrier, inc=1, device_id=target, device_id_type=pl.DeviceIdType.MESH
        )
    pl.semaphore_wait(barrier, count - 1)

    def send(source, destination, send_at, recv_at, target):
        copy = pltpu.make_async_remote_copy(
            src_ref=source,
            dst_ref=destination,
            send_sem=send_at,
            recv_sem=recv_at,
            device_id=target,
            device_id_type=pl.DeviceIdType.MESH,
        )
        copy.start()
        return copy

    ends = (others[0], others[-1])
    first = [
        send(share_ref.at[k], shares.at[k], share_send.at[k], share_recv.at[k], ends[k])
        for k in range(2)
    ]
    rims = [
        send(source, destination, rim_send.at[k], rim_recv.at[k], ends[k])
        for k, (source, destination) in enumerate(((up_ref, up_in), (low_ref, low_in)))
    ]
    for copy in first:
        copy.wait()
    subs = part_ref.shape[0]
    for sub in range(subs):
        value = part_ref[sub]
        if sub == 0:
            value = value + shares[0]
        if sub == subs - 1:
            value = value + shares[1]
        all_ref[me, sub] = value.astype(bf16)
    pushes = [
        send(all_ref.at[me], all_ref.at[me], send_sem.at[k], recv_sem.at[k], target)
        for k, target in enumerate(others)
    ]
    for copy in pushes + rims:
        copy.wait()


def exchange(part, share, up, low, collective_id):
    count = lax.axis_size("dom")
    vmem = pl.BlockSpec(memory_space=pltpu.VMEM)
    return pl.pallas_call(
        functools.partial(exchange_kernel, count),
        out_shape=[
            jax.ShapeDtypeStruct((count,) + part.shape, bf16),
            jax.ShapeDtypeStruct(up.shape, up.dtype),
            jax.ShapeDtypeStruct(low.shape, low.dtype),
        ],
        in_specs=[vmem] * 4,
        out_specs=[vmem] * 3,
        scratch_shapes=[pltpu.VMEM(share.shape, f32)]
        + [pltpu.SemaphoreType.DMA((2,))] * 4
        + [pltpu.SemaphoreType.DMA((count - 1,))] * 2,
        compiler_params=pltpu.CompilerParams(collective_id=collective_id, has_side_effects=True),
    )(part, share, up, low)


def put_split(ref, rows, value):
    width = value.shape[1]
    high = value.astype(bf16)
    ref[rows, :width] = high
    ref[rows, width:] = (value - high.astype(f32)).astype(bf16)


def joined_halves(pair):
    width = pair.shape[1] // 2
    return pair[:, :width] + pair[:, width:]


def setup_kernel(row_ref, col_ref, a_ref, out_ref, diagonal_ref, rest, table, diagonal):
    depth, size = out_ref.shape

    @pl.when(pl.program_id(1) == 0)
    def _():
        spots = row_ref[...]
        diagonal[...] = jnp.zeros_like(diagonal)

        @pl.loop(0, size // depth)
        def _(b):
            start = pl.multiple_of(b * depth, depth)
            row = lax.broadcasted_iota(jnp.int32, (depth, size), 0) + start
            same = row == lax.broadcasted_iota(jnp.int32, (depth, size), 1)
            block = a_ref[pl.ds(start, depth), :]
            diagonal[...] += jnp.sum(jnp.where(same, block, 0.0), axis=0, keepdims=True)
            rest[pl.ds(start, depth), :] = jnp.where(same, 0.0, block).astype(bf16)
            table[pl.ds(start, depth), :] = jnp.where(row == spots, 1.0, 0.0).astype(bf16)

    hit = lax.broadcasted_iota(jnp.int32, (depth, size), 1) == col_ref[...]
    diagonal_ref[...] = jnp.sum(jnp.where(hit, diagonal[...], 0.0), axis=1, keepdims=True)
    picked = jnp.dot(
        jnp.where(hit, 1.0, 0.0).astype(bf16), rest[...], preferred_element_type=f32
    ).astype(bf16)
    out_ref[...] = jnp.dot(picked, table[...], preferred_element_type=f32).astype(bf16)


def slot_operator(dual_ops, row_perm, col_perm, sub):
    size = dual_ops.shape[1]
    depth = next(d for d in (256, 128, 64, 32, 16) if size % d == 0)
    return pl.pallas_call(
        setup_kernel,
        grid=(1, size // depth),
        out_shape=[
            jax.ShapeDtypeStruct((size, size), bf16),
            jax.ShapeDtypeStruct((size, 1), f32),
        ],
        in_specs=[
            pl.BlockSpec((None, 1, size), lambda s, i: (sub, 0, 0)),
            pl.BlockSpec((None, depth, 1), lambda s, i: (sub, i, 0)),
            pl.BlockSpec((None, size, size), lambda s, i: (sub, 0, 0)),
        ],
        out_specs=[
            pl.BlockSpec((depth, size), lambda s, i: (i, 0)),
            pl.BlockSpec((depth, 1), lambda s, i: (i, 0)),
        ],
        scratch_shapes=[
            pltpu.VMEM((size, size), bf16),
            pltpu.VMEM((size, size), bf16),
            pltpu.VMEM((1, size), f32),
        ],
        cost_estimate=pl.CostEstimate(
            flops=4 * size**3, bytes_accessed=6 * size * size, transcendentals=0
        ),
        compiler_params=pltpu.CompilerParams(vmem_limit_bytes=56 * 2**20),
    )(row_perm, col_perm, dual_ops)


def apply_kernel(sub, d_ref, a_ref, lower_ref, upper_ref, lower_low_ref, upper_low_ref, xs):
    half = a_ref.shape[0]
    step = pl.program_id(0)

    @pl.when(step == 0)
    def _():
        put_split(xs, pl.ds(0, half), -d_ref[sub])
        put_split(xs, pl.ds(half, half), d_ref[sub + 1])

    outs = ((lower_ref, lower_low_ref), (upper_ref, upper_low_ref))
    depth = half // 3 if half % 48 == 0 else half
    for side, (wide, narrow) in enumerate(outs):

        @pl.when(step == side)
        def _():
            for start in range(0, half, depth):
                rows = pl.ds(start, depth)
                value = joined_halves(
                    jnp.dot(a_ref[rows, :], xs[...], preferred_element_type=f32)
                )
                wide[rows, :] = value
                narrow[rows, :] = value.astype(bf16)


def apply_operator(direction, operator, sub):
    size = operator.shape[0]
    half, width = direction.shape[1:]
    return pl.pallas_call(
        functools.partial(apply_kernel, sub),
        grid=(2,),
        out_shape=[jax.ShapeDtypeStruct((half, width), f32)] * 2
        + [jax.ShapeDtypeStruct((half, width), bf16)] * 2,
        in_specs=[
            pl.BlockSpec(direction.shape, lambda i: (0, 0, 0)),
            pl.BlockSpec((half, size), lambda i: (i, 0)),
        ],
        out_specs=[pl.BlockSpec((half, width), lambda i: (0, 0))] * 4,
        scratch_shapes=[pltpu.VMEM((size, 2 * width), bf16)],
        cost_estimate=pl.CostEstimate(
            flops=4 * size * size * width, bytes_accessed=2 * size * size, transcendentals=0
        ),
        compiler_params=pltpu.CompilerParams(vmem_limit_bytes=24 * 2**20),
    )(direction, operator)


def split(value, axis):
    high = lax.reduce_precision(value, 8, 7)
    return jnp.concatenate([high.astype(bf16), (value - high).astype(bf16)], axis=axis)


def unsplit(pair):
    width = pair.shape[-1] // 2
    return pair[..., :width] + pair[..., width:]


def shards(dual_ops, modes, coarse_rows, coarse_cols, row_perm, iface_size, rhs):
    sub_count, half_width, case_count = rhs.shape
    size = 2 * half_width
    mode_count = modes.shape[1]
    dom_count = lax.axis_size("dom") * sub_count
    row_view = row_perm[:, None, :]
    col_view = row_perm[:, :, None]
    block_count = coarse_cols.shape[1]
    int_pack = jnp.concatenate([coarse_cols, iface_size[:, None]], axis=1)
    live_own = (
        lax.broadcasted_iota(jnp.int32, (sub_count, half_width), 1) < iface_size[:, None]
    ).astype(f32)[:, :, None]
    start_vector = rhs * live_own
    prior_rim = from_behind(start_vector[-1], "dom", 1)
    prior_ints = from_behind(int_pack[-1], "dom", 1)
    next_ints = from_behind(int_pack[0], "dom", -1)
    permutation = (
        row_perm[:, :, None] == lax.broadcasted_iota(jnp.int32, (1, 1, size), 2)
    ).astype(bf16)
    slot_modes = jnp.einsum("sjn,skn->sjk", modes, permutation, preferred_element_type=f32).astype(
        bf16
    )
    prior_modes = from_behind(slot_modes[-1], "dom", 1)
    next_modes = from_behind(slot_modes[0], "dom", -1)
    prior_blocks = from_behind(coarse_rows[-1], "dom", 1)
    next_blocks = from_behind(coarse_rows[0], "dom", -1)
    ext_ints = jnp.concatenate([prior_ints[None], int_pack, next_ints[None]], axis=0)
    ext_cols = ext_ints[:, :block_count]
    ext_size = ext_ints[:-1, block_count]
    ext_modes = jnp.concatenate([prior_modes[None], slot_modes, next_modes[None]], axis=0)
    ext_blocks = jnp.concatenate([prior_blocks[None], coarse_rows, next_blocks[None]], axis=0)
    live = (
        lax.broadcasted_iota(jnp.int32, (sub_count + 1, half_width), 1) < ext_size[:, None]
    ).astype(f32)[:, :, None]
    operators, diagonals = zip(
        *[slot_operator(dual_ops, row_view, col_view, sub) for sub in range(sub_count)]
    )
    upper_diagonals = [d[half_width:, 0] for d in diagonals]
    lower_diagonals = [d[:half_width, 0] for d in diagonals]
    upper_diagonals = [from_behind(upper_diagonals[-1], "dom", 1)] + upper_diagonals
    lower_diagonals = lower_diagonals + [from_behind(lower_diagonals[0], "dom", -1)]
    diagonal = jnp.stack(upper_diagonals) + jnp.stack(lower_diagonals)
    diagonal = diagonal[:, :, None]
    column_table = (
        ext_cols[:, :, None] == lax.broadcasted_iota(jnp.int32, (1, 1, dom_count), 2)
    ).astype(f32)
    coarse = jnp.einsum("sqij,sqd->sidj", ext_blocks, column_table, precision=highest).reshape(
        (sub_count + 2) * mode_count, dom_count * mode_count
    )
    fit_modes = jnp.concatenate([-slot_modes[:, :, :half_width], slot_modes[:, :, half_width:]], 2)
    join_modes = jnp.concatenate(
        [ext_modes[:-1, :, half_width:], -ext_modes[1:, :, :half_width]], axis=1
    )

    def fit(vector):
        pairs = split(vector, 2)
        locals_ = jnp.concatenate([pairs[:-1], pairs[1:]], axis=1)
        return unsplit(jnp.einsum("sjn,snc->sjc", fit_modes, locals_, preferred_element_type=f32))

    share_modes = jnp.stack([-ext_modes[-1, :, :half_width], -ext_modes[0, :, half_width:]])

    def correction_of(everyone):
        everyone = everyone.reshape(dom_count * mode_count, case_count)
        amounts = jnp.dot(coarse, everyone.astype(f32), precision=highest)
        amounts = split(amounts, 1).reshape(sub_count + 2, mode_count, 2 * case_count)
        amounts = jnp.concatenate([amounts[:-1], amounts[1:]], axis=1)
        return live * unsplit(
            jnp.einsum("sjn,sjc->snc", join_modes, amounts, preferred_element_type=f32)
        )

    centre = 0.5 * (high_bound + low_bound)
    radius = 0.5 * (high_bound - low_bound)
    spread_ratio = centre / radius
    ratio_now = 1.0 / spread_ratio
    residual = jnp.concatenate([prior_rim[None], start_vector], axis=0)
    residual = residual - correction_of(push_gather(fit(residual).astype(bf16), ("dom",), 1))
    direction = residual / centre
    solution = jnp.zeros_like(rhs)
    sums = []
    for turn_index in range(STEPS):
        solution = solution + direction[1:]
        lowers, uppers = [None] * sub_count, [None] * sub_count
        order = [sub_count - 1] + list(range(sub_count - 1))
        for sub in order:
            lower, upper, lower_low, upper_low = apply_operator(direction, operators[sub], sub)
            lowers[sub], uppers[sub] = lower, upper
            if sub == sub_count - 1:
                up_low = upper_low
            if sub == 0:
                low_low = lower_low
        none = jnp.zeros_like(lowers[0])
        rest = jnp.stack([u - l for u, l in zip([none] + uppers, lowers + [none])])
        mapped = (diagonal * direction + rest) * live
        ends = jnp.stack([uppers[-1] * live[-1], lowers[0] * live[0]])
        share = unsplit(
            jnp.einsum("sjn,snc->sjc", share_modes, split(ends, 2), preferred_element_type=f32)
        )
        everyone, rim_up, rim_low = exchange(fit(mapped), share, up_low, low_low, 3)
        mapped = mapped.at[0].add(rim_up.astype(f32) * live[0])
        mapped = mapped.at[-1].add(-rim_low.astype(f32) * live[-1])
        residual = residual - (mapped - correction_of(everyone))
        sums.append(jnp.sum(residual[1:] * residual[1:], axis=(0, 1)))
        if turn_index + 1 < STEPS:
            ratio_next = 1.0 / (2.0 * spread_ratio - ratio_now)
            direction = ratio_next * ratio_now * direction + 2.0 * ratio_next / radius * residual
            ratio_now = ratio_next
    rows = -(-STEPS // 8) * 8
    pack = jnp.zeros((rows, case_count), f32).at[:STEPS].set(jnp.stack(sums))
    cases = lax.axis_size("case")
    everyone = push_gather(pack, ("dom", "case"), 2).reshape(-1, cases, rows, case_count)
    norms = jnp.sqrt(jnp.sum(everyone, axis=0)[:, :STEPS] + epsilon)
    history = lax.dynamic_index_in_dim(norms, lax.axis_index("case"), 0, keepdims=False)
    peak_norm = jnp.max(norms, axis=(0, 2))
    return (solution, residual[1:], history, peak_norm)


def solution(mesh):
    in_specs = (
        P("dom", None, None),
        P("dom", None, None),
        P("dom", None, None, None),
        P("dom", None),
        P("dom", None),
        P("dom"),
        P("dom", None, "case"),
    )
    out_specs = (P("dom", None, "case"), P("dom", None, "case"), P(None, "case"), P())
    return jax.shard_map(shards, mesh=mesh, in_specs=in_specs, out_specs=out_specs, check_vma=False)
```

```python
import functools

import jax
import jax.numpy as jnp
from jax import lax
from jax.experimental import pallas as pl
from jax.experimental.pallas import tpu as pltpu
from jax.sharding import PartitionSpec as P

STEPS = 4


low_bound = 2.0
high_bound = 14.0
epsilon = 1e-06
highest = lax.Precision.HIGHEST
f32, bf16 = jnp.float32, jnp.bfloat16


def from_behind(block, axis, distance):
    devices = range(lax.axis_size(axis))
    route = [((i - distance) % len(devices), i) for i in devices]
    return lax.ppermute(block, axis, route)


def gather_kernel(axes, sizes, x_ref, out_ref, own_sem, send_sem, recv_sem):
    me = [lax.axis_index(axis) for axis in axes]

    def flat(position):
        index = 0
        for at, size in zip(position, sizes):
            index = index * size + at
        return index

    offsets = [()]
    for size in sizes:
        offsets = [o + (k,) for o in offsets for k in range(size)]
    targets = [
        {axis: lax.rem(at + k, size) for axis, at, k, size in zip(axes, me, offset, sizes)}
        for offset in offsets[1:]
    ]
    barrier = pltpu.get_barrier_semaphore()
    for target in targets:
        pl.semaphore_signal(
            barrier, inc=1, device_id=target, device_id_type=pl.DeviceIdType.MESH
        )
    own = pltpu.make_async_copy(x_ref, out_ref.at[flat(me)], own_sem)
    own.start()
    pl.semaphore_wait(barrier, len(targets))
    copies = []
    for k, target in enumerate(targets):
        copy = pltpu.make_async_remote_copy(
            src_ref=x_ref,
            dst_ref=out_ref.at[flat(me)],
            send_sem=send_sem.at[k],
            recv_sem=recv_sem.at[k],
            device_id=target,
            device_id_type=pl.DeviceIdType.MESH,
        )
        copy.start()
        copies.append(copy)
    own.wait()
    for copy in copies:
        copy.wait()


def push_gather(block, axes, collective_id):
    sizes = tuple(lax.axis_size(axis) for axis in axes)
    count = 1
    for size in sizes:
        count *= size
    return pl.pallas_call(
        functools.partial(gather_kernel, axes, sizes),
        out_shape=jax.ShapeDtypeStruct((count,) + block.shape, block.dtype),
        in_specs=[pl.BlockSpec(memory_space=pltpu.VMEM)],
        out_specs=pl.BlockSpec(memory_space=pltpu.VMEM),
        scratch_shapes=[
            pltpu.SemaphoreType.DMA,
            pltpu.SemaphoreType.DMA((count - 1,)),
            pltpu.SemaphoreType.DMA((count - 1,)),
        ],
        compiler_params=pltpu.CompilerParams(collective_id=collective_id, has_side_effects=True),
    )(block)


def exchange_kernel(
    count, part_ref, share_ref, up_ref, low_ref, all_ref, up_in, low_in, shares,
    share_send, share_recv, rim_send, rim_recv, send_sem, recv_sem
):
    me = lax.axis_index("dom")
    others = [{"dom": lax.rem(me + k, count)} for k in range(1, count)]
    barrier = pltpu.get_barrier_semaphore()
    for target in others:
        pl.semaphore_signal(
            barrier, inc=1, device_id=target, device_id_type=pl.DeviceIdType.MESH
        )
    pl.semaphore_wait(barrier, count - 1)

    def send(source, destination, send_at, recv_at, target):
        copy = pltpu.make_async_remote_copy(
            src_ref=source,
            dst_ref=destination,
            send_sem=send_at,
            recv_sem=recv_at,
            device_id=target,
            device_id_type=pl.DeviceIdType.MESH,
        )
        copy.start()
        return copy

    ends = (others[0], others[-1])
    first = [
        send(share_ref.at[k], shares.at[k], share_send.at[k], share_recv.at[k], ends[k])
        for k in range(2)
    ]
    rims = [
        send(source, destination, rim_send.at[k], rim_recv.at[k], ends[k])
        for k, (source, destination) in enumerate(((up_ref, up_in), (low_ref, low_in)))
    ]
    for copy in first:
        copy.wait()
    subs = part_ref.shape[0]
    for sub in range(subs):
        value = part_ref[sub]
        if sub == 0:
            value = value + shares[0]
        if sub == subs - 1:
            value = value + shares[1]
        all_ref[me, sub] = value.astype(bf16)
    pushes = [
        send(all_ref.at[me], all_ref.at[me], send_sem.at[k], recv_sem.at[k], target)
        for k, target in enumerate(others)
    ]
    for copy in pushes + rims:
        copy.wait()


def exchange(part, share, up, low, collective_id):
    count = lax.axis_size("dom")
    vmem = pl.BlockSpec(memory_space=pltpu.VMEM)
    return pl.pallas_call(
        functools.partial(exchange_kernel, count),
        out_shape=[
            jax.ShapeDtypeStruct((count,) + part.shape, bf16),
            jax.ShapeDtypeStruct(up.shape, up.dtype),
            jax.ShapeDtypeStruct(low.shape, low.dtype),
        ],
        in_specs=[vmem] * 4,
        out_specs=[vmem] * 3,
        scratch_shapes=[pltpu.VMEM(share.shape, f32)]
        + [pltpu.SemaphoreType.DMA((2,))] * 4
        + [pltpu.SemaphoreType.DMA((count - 1,))] * 2,
        compiler_params=pltpu.CompilerParams(collective_id=collective_id, has_side_effects=True),
    )(part, share, up, low)


def put_split(ref, rows, value):
    width = value.shape[1]
    high = value.astype(bf16)
    ref[rows, :width] = high
    ref[rows, width:] = (value - high.astype(f32)).astype(bf16)


def joined_halves(pair):
    width = pair.shape[1] // 2
    return pair[:, :width] + pair[:, width:]


def setup_kernel(row_ref, col_ref, a_ref, out_ref, diagonal_ref, rest, table, diagonal):
    depth, size = out_ref.shape

    @pl.when(pl.program_id(1) == 0)
    def _():
        spots = row_ref[...]
        diagonal[...] = jnp.zeros_like(diagonal)

        @pl.loop(0, size // depth)
        def _(b):
            start = pl.multiple_of(b * depth, depth)
            row = lax.broadcasted_iota(jnp.int32, (depth, size), 0) + start
            same = row == lax.broadcasted_iota(jnp.int32, (depth, size), 1)
            block = a_ref[pl.ds(start, depth), :]
            diagonal[...] += jnp.sum(jnp.where(same, block, 0.0), axis=0, keepdims=True)
            rest[pl.ds(start, depth), :] = jnp.where(same, 0.0, block).astype(bf16)
            table[pl.ds(start, depth), :] = jnp.where(row == spots, 1.0, 0.0).astype(bf16)

    hit = lax.broadcasted_iota(jnp.int32, (depth, size), 1) == col_ref[...]
    diagonal_ref[...] = jnp.sum(jnp.where(hit, diagonal[...], 0.0), axis=1, keepdims=True)
    picked = jnp.dot(
        jnp.where(hit, 1.0, 0.0).astype(bf16), rest[...], preferred_element_type=f32
    ).astype(bf16)
    out_ref[...] = jnp.dot(picked, table[...], preferred_element_type=f32).astype(bf16)


def slot_operator(dual_ops, row_perm, col_perm, sub):
    size = dual_ops.shape[1]
    depth = next(d for d in (256, 128, 64, 32, 16) if size % d == 0)
    return pl.pallas_call(
        setup_kernel,
        grid=(1, size // depth),
        out_shape=[
            jax.ShapeDtypeStruct((size, size), bf16),
            jax.ShapeDtypeStruct((size, 1), f32),
        ],
        in_specs=[
            pl.BlockSpec((None, 1, size), lambda s, i: (sub, 0, 0)),
            pl.BlockSpec((None, depth, 1), lambda s, i: (sub, i, 0)),
            pl.BlockSpec((None, size, size), lambda s, i: (sub, 0, 0)),
        ],
        out_specs=[
            pl.BlockSpec((depth, size), lambda s, i: (i, 0)),
            pl.BlockSpec((depth, 1), lambda s, i: (i, 0)),
        ],
        scratch_shapes=[
            pltpu.VMEM((size, size), bf16),
            pltpu.VMEM((size, size), bf16),
            pltpu.VMEM((1, size), f32),
        ],
        cost_estimate=pl.CostEstimate(
            flops=4 * size**3, bytes_accessed=6 * size * size, transcendentals=0
        ),
        compiler_params=pltpu.CompilerParams(vmem_limit_bytes=56 * 2**20),
    )(row_perm, col_perm, dual_ops)


def apply_kernel(sub, d_ref, a_ref, lower_ref, upper_ref, lower_low_ref, upper_low_ref, xs):
    half = a_ref.shape[0]
    step = pl.program_id(0)

    @pl.when(step == 0)
    def _():
        put_split(xs, pl.ds(0, half), -d_ref[sub])
        put_split(xs, pl.ds(half, half), d_ref[sub + 1])

    outs = ((lower_ref, lower_low_ref), (upper_ref, upper_low_ref))
    depth = half // 3 if half % 48 == 0 else half
    for side, (wide, narrow) in enumerate(outs):

        @pl.when(step == side)
        def _():
            for start in range(0, half, depth):
                rows = pl.ds(start, depth)
                value = joined_halves(
                    jnp.dot(a_ref[rows, :], xs[...], preferred_element_type=f32)
                )
                wide[rows, :] = value
                narrow[rows, :] = value.astype(bf16)


def apply_operator(direction, operator, sub):
    size = operator.shape[0]
    half, width = direction.shape[1:]
    return pl.pallas_call(
        functools.partial(apply_kernel, sub),
        grid=(2,),
        out_shape=[jax.ShapeDtypeStruct((half, width), f32)] * 2
        + [jax.ShapeDtypeStruct((half, width), bf16)] * 2,
        in_specs=[
            pl.BlockSpec(direction.shape, lambda i: (0, 0, 0)),
            pl.BlockSpec((half, size), lambda i: (i, 0)),
        ],
        out_specs=[pl.BlockSpec((half, width), lambda i: (0, 0))] * 4,
        scratch_shapes=[pltpu.VMEM((size, 2 * width), bf16)],
        cost_estimate=pl.CostEstimate(
            flops=4 * size * size * width, bytes_accessed=2 * size * size, transcendentals=0
        ),
        compiler_params=pltpu.CompilerParams(vmem_limit_bytes=24 * 2**20),
    )(direction, operator)


def split(value, axis):
    high = lax.reduce_precision(value, 8, 7)
    return jnp.concatenate([high.astype(bf16), (value - high).astype(bf16)], axis=axis)


def unsplit(pair):
    width = pair.shape[-1] // 2
    return pair[..., :width] + pair[..., width:]


def shards(dual_ops, modes, coarse_rows, coarse_cols, row_perm, iface_size, rhs):
    sub_count, half_width, case_count = rhs.shape
    size = 2 * half_width
    mode_count = modes.shape[1]
    dom_count = lax.axis_size("dom") * sub_count
    row_view = row_perm[:, None, :]
    col_view = row_perm[:, :, None]
    block_count = coarse_cols.shape[1]
    int_pack = jnp.concatenate([coarse_cols, iface_size[:, None]], axis=1)
    live_own = (
        lax.broadcasted_iota(jnp.int32, (sub_count, half_width), 1) < iface_size[:, None]
    ).astype(f32)[:, :, None]
    start_vector = rhs * live_own
    prior_rim = from_behind(start_vector[-1], "dom", 1)
    prior_ints = from_behind(int_pack[-1], "dom", 1)
    next_ints = from_behind(int_pack[0], "dom", -1)
    permutation = (
        row_perm[:, :, None] == lax.broadcasted_iota(jnp.int32, (1, 1, size), 2)
    ).astype(bf16)
    slot_modes = jnp.einsum("sjn,skn->sjk", modes, permutation, preferred_element_type=f32).astype(
        bf16
    )
    prior_modes = from_behind(slot_modes[-1], "dom", 1)
    next_modes = from_behind(slot_modes[0], "dom", -1)
    prior_blocks = from_behind(coarse_rows[-1], "dom", 1)
    next_blocks = from_behind(coarse_rows[0], "dom", -1)
    ext_ints = jnp.concatenate([prior_ints[None], int_pack, next_ints[None]], axis=0)
    ext_cols = ext_ints[:, :block_count]
    ext_size = ext_ints[:-1, block_count]
    ext_modes = jnp.concatenate([prior_modes[None], slot_modes, next_modes[None]], axis=0)
    ext_blocks = jnp.concatenate([prior_blocks[None], coarse_rows, next_blocks[None]], axis=0)
    live = (
        lax.broadcasted_iota(jnp.int32, (sub_count + 1, half_width), 1) < ext_size[:, None]
    ).astype(f32)[:, :, None]
    operators, diagonals = zip(
        *[slot_operator(dual_ops, row_view, col_view, sub) for sub in range(sub_count)]
    )
    upper_diagonals = [d[half_width:, 0] for d in diagonals]
    lower_diagonals = [d[:half_width, 0] for d in diagonals]
    upper_diagonals = [from_behind(upper_diagonals[-1], "dom", 1)] + upper_diagonals
    lower_diagonals = lower_diagonals + [from_behind(lower_diagonals[0], "dom", -1)]
    diagonal = jnp.stack(upper_diagonals) + jnp.stack(lower_diagonals)
    diagonal = diagonal[:, :, None]
    column_table = (
        ext_cols[:, :, None] == lax.broadcasted_iota(jnp.int32, (1, 1, dom_count), 2)
    ).astype(f32)
    coarse = jnp.einsum("sqij,sqd->sidj", ext_blocks, column_table, precision=highest).reshape(
        (sub_count + 2) * mode_count, dom_count * mode_count
    )
    fit_modes = jnp.concatenate([-slot_modes[:, :, :half_width], slot_modes[:, :, half_width:]], 2)
    join_modes = jnp.concatenate(
        [ext_modes[:-1, :, half_width:], -ext_modes[1:, :, :half_width]], axis=1
    )

    def fit(vector):
        pairs = split(vector, 2)
        locals_ = jnp.concatenate([pairs[:-1], pairs[1:]], axis=1)
        return unsplit(jnp.einsum("sjn,snc->sjc", fit_modes, locals_, preferred_element_type=f32))

    share_modes = jnp.stack([-ext_modes[-1, :, :half_width], -ext_modes[0, :, half_width:]])

    def correction_of(everyone):
        everyone = everyone.reshape(dom_count * mode_count, case_count)
        amounts = jnp.dot(coarse, everyone.astype(f32), precision=highest)
        amounts = split(amounts, 1).reshape(sub_count + 2, mode_count, 2 * case_count)
        amounts = jnp.concatenate([amounts[:-1], amounts[1:]], axis=1)
        return live * unsplit(
            jnp.einsum("sjn,sjc->snc", join_modes, amounts, preferred_element_type=f32)
        )

    centre = 0.5 * (high_bound + low_bound)
    radius = 0.5 * (high_bound - low_bound)
    spread_ratio = centre / radius
    ratio_now = 1.0 / spread_ratio
    residual = jnp.concatenate([prior_rim[None], start_vector], axis=0)
    residual = residual - correction_of(push_gather(fit(residual).astype(bf16), ("dom",), 1))
    direction = residual / centre
    solution = jnp.zeros_like(rhs)
    sums = []
    for turn_index in range(STEPS):
        solution = solution + direction[1:]
        lowers, uppers = [None] * sub_count, [None] * sub_count
        order = [sub_count - 1] + list(range(sub_count - 1))
        for sub in order:
            lower, upper, lower_low, upper_low = apply_operator(direction, operators[sub], sub)
            lowers[sub], uppers[sub] = lower, upper
            if sub == sub_count - 1:
                up_low = upper_low
            if sub == 0:
                low_low = lower_low
        none = jnp.zeros_like(lowers[0])
        rest = jnp.stack([u - l for u, l in zip([none] + uppers, lowers + [none])])
        mapped = (diagonal * direction + rest) * live
        ends = jnp.stack([uppers[-1] * live[-1], lowers[0] * live[0]])
        share = unsplit(
            jnp.einsum("sjn,snc->sjc", share_modes, split(ends, 2), preferred_element_type=f32)
        )
        everyone, rim_up, rim_low = exchange(fit(mapped), share, up_low, low_low, 3)
        before = [rim_up.astype(f32)] + uppers
        after = lowers + [rim_low.astype(f32)]
        rest = jnp.stack([u - l for u, l in zip(before, after)])
        mapped = (diagonal * direction + rest) * live
        residual = residual - (mapped - correction_of(everyone))
        sums.append(jnp.sum(residual[1:] * residual[1:], axis=(0, 1)))
        if turn_index + 1 < STEPS:
            ratio_next = 1.0 / (2.0 * spread_ratio - ratio_now)
            direction = ratio_next * ratio_now * direction + 2.0 * ratio_next / radius * residual
            ratio_now = ratio_next
    rows = -(-STEPS // 8) * 8
    pack = jnp.zeros((rows, case_count), f32).at[:STEPS].set(jnp.stack(sums))
    cases = lax.axis_size("case")
    everyone = push_gather(pack, ("dom", "case"), 2).reshape(-1, cases, rows, case_count)
    norms = jnp.sqrt(jnp.sum(everyone, axis=0)[:, :STEPS] + epsilon)
    history = lax.dynamic_index_in_dim(norms, lax.axis_index("case"), 0, keepdims=False)
    peak_norm = jnp.max(norms, axis=(0, 2))
    return (solution, residual[1:], history, peak_norm)


def solution(mesh):
    in_specs = (
        P("dom", None, None),
        P("dom", None, None),
        P("dom", None, None, None),
        P("dom", None),
        P("dom", None),
        P("dom"),
        P("dom", None, "case"),
    )
    out_specs = (P("dom", None, "case"), P("dom", None, "case"), P(None, "case"), P())
    return jax.shard_map(shards, mesh=mesh, in_specs=in_specs, out_specs=out_specs, check_vma=False)
```
